32 devices in a mesh: groups: 1, replica: 32 (over z, y, x, core).
Axes of the slice: x: 2, y: 2, z: 4, core: 2. Of those that a mesh axis runs over, the one named last changes fastest.
Arguments:
- queries: bfloat16 [8192, 1024], P(('groups', 'replica')), may hold values from -15 to 15
- suffix_kv: bfloat16 [8192, 256], P(('groups', 'replica')), may hold values from -6 to 6
- own_cache: bfloat16 [16384, 256], P(('groups', 'replica')), may hold values from -6 to 6
- ctx_len: int32 [32], P(('groups', 'replica')), may hold values from 64 to 512, as said below
- prefix_cache: bfloat16 [131072, 256], P(('groups', 'replica')), may hold values from -18 to 18
- owners: int32 [2], P('groups'), may hold values from 0 to 31, as said below
- readers: int32 [32], P('groups'), may hold values from 0 to 1
- kv_pool: bfloat16 [1024, 128, 256], P(('groups', 'replica')), may hold values from -6 to 6
- mig_target: int32 [32, 32], P(('groups', 'replica')), may hold values from 0 to 31, as said below
- mig_block: int32 [32, 32], P(('groups', 'replica')), may hold values from 0 to 31, each once within a row
- mig_count: int32 [32], P(('groups', 'replica')), may hold values from 8 to 32, as said below
Outputs:
- attended: bfloat16 [8192, 1024], P(('groups', 'replica'))
The draws below stay inside these ranges and needn't reach their ends.
Inputs may be any that keep to these rules, and one draw needn't show every extreme that they name: `owners`: 2 different replicas; replica 32 - 1 owns one prefix in every draw. `ctx_len`: the largest value is 512 in every draw. `mig_target`: each row names every replica once, so one source sends at most one block to one target; in every draw one replica is the first entry of every row. `mig_block`: each row names every block of the source's pool once. `mig_count`: the largest value is 32 in every draw.
All inputs are finite; a program needn't handle non-finite values.
Results may differ from the reference program's by a relative error of at most 0.0019.
Values may be sent and summed in bfloat16 or wider, within the bound.
A program may use at most 128 MiB of HBM per device.

```python
import math
import jax
import jax.numpy as jnp
import numpy as np
from jax import lax

HD = 128
HQ = 8
SUF = 256
PL = 4096
CTX = 512
BLK = 128
NP = 2
NB = 32
N_REPLICA = 32


def sign_pattern(key):
    flips = jax.random.bernoulli(jax.random.fold_in(key, 991), 0.5, (HD,))
    return jnp.where(flips, 1.0, -1.0).astype(jnp.float32)


def crossing_pattern(key):
    balanced = jnp.where(jnp.arange(HD) < HD // 2, 1.0, -1.0).astype(jnp.float32)
    mixed = jax.random.permutation(jax.random.fold_in(key, 993), balanced)
    return (sign_pattern(key) * mixed).astype(jnp.float32)


def column_scale():
    return jnp.where(jnp.arange(2 * HD) < HD, 0.6, 1.0).astype(jnp.float32)


def cache_rows(key, salt, shape):
    drawn = jnp.clip(jax.random.normal(jax.random.fold_in(key, salt), shape, jnp.float32), -6.0, 6.0)
    return (drawn * column_scale()).astype(jnp.bfloat16)


def draw_suffix_kv(key, part):
    return cache_rows(key, 41, (N_REPLICA * SUF, 2 * HD))


def draw_own_cache(key, part):
    return cache_rows(key, 43, (N_REPLICA * CTX, 2 * HD))


def draw_kv_pool(key, part):
    return cache_rows(key, 47, (N_REPLICA * NB, BLK, 2 * HD))


def draw_queries(key, part):
    drawn = jnp.clip(4.0 * jax.random.normal(jax.random.fold_in(key, 11), (N_REPLICA, SUF, HQ, HD), jnp.float32), -15.0, 15.0)
    return drawn.reshape(N_REPLICA * SUF, HQ * HD).astype(jnp.bfloat16)


def draw_prefix_cache(key, part):
    drawn = jnp.clip(jax.random.normal(jax.random.fold_in(key, 23), (N_REPLICA, PL, 2 * HD), jnp.float32), -6.0, 6.0)
    drawn = drawn * column_scale()[None, None, :]
    planted = jax.random.randint(jax.random.fold_in(key, 53), (N_REPLICA,), 2, PL).astype(jnp.int32)
    rows = jnp.arange(PL, dtype=jnp.int32)
    columns = jnp.arange(2 * HD, dtype=jnp.int32)
    large_key = jnp.concatenate([18.0 * crossing_pattern(key), jnp.zeros((HD,), jnp.float32)])
    select = (rows[None, :, None] == planted[:, None, None]) & (columns[None, None, :] < HD)
    drawn = jnp.where(select, large_key[None, None, :], drawn)
    return drawn.reshape(N_REPLICA * PL, 2 * HD).astype(jnp.bfloat16)


def draw_owners(key, part):
    others = jax.random.permutation(jax.random.fold_in(key, 31), N_REPLICA - 1)[:NP - 1].astype(jnp.int32)
    listed = jnp.concatenate([others, jnp.full((1,), N_REPLICA - 1, jnp.int32)])
    order = jax.random.permutation(jax.random.fold_in(key, 37), NP)
    return listed[order].astype(jnp.int32)


def draw_ctx_len(key, part):
    lengths = jax.random.randint(jax.random.fold_in(key, 3), (N_REPLICA,), CTX // 8, CTX + 1).astype(jnp.int32)
    picked = jax.random.randint(jax.random.fold_in(key, 4), (), 0, N_REPLICA)
    return lengths.at[picked].set(CTX).astype(jnp.int32)


def draw_mig_target(key, part):
    first = jax.random.randint(jax.random.fold_in(key, 5), (), 0, N_REPLICA)
    columns = jnp.arange(N_REPLICA, dtype=jnp.int32)
    ranking = jax.random.randint(jax.random.fold_in(key, 6), (N_REPLICA, N_REPLICA), 0, 2 ** 20) * N_REPLICA + columns[None, :]
    ranking = jnp.where(columns[None, :] == first, -1, ranking)
    return jnp.argsort(ranking, axis=1, stable=True).astype(jnp.int32)


def draw_mig_count(key, part):
    counts = jax.random.randint(jax.random.fold_in(key, 7), (N_REPLICA,), N_REPLICA // 4, N_REPLICA + 1).astype(jnp.int32)
    picked = jax.random.randint(jax.random.fold_in(key, 8), (), 0, N_REPLICA)
    return counts.at[picked].set(N_REPLICA).astype(jnp.int32)


def plant(values, rng, least, top_value):
    extent = values.shape
    place = [jax.random.randint(jax.random.fold_in(rng, axis), (), 0, extent[axis]) for axis in range(len(extent))]
    values = values.at[tuple(place)].set(least)
    longest = extent.index(max(extent))
    place[longest] = (place[longest] + 1) % extent[longest]
    return values.at[tuple(place)].set(top_value)


def rank_bounds(count, lean):
    weights = [(1 << 20) // math.isqrt(rank ** lean) + 1 for rank in range(1, count + 1)]
    width = 1 + sum(weights) // (1 << 30)
    return np.cumsum(np.array([max(1, weight // width) for weight in weights]))


def ranked(key, extent, count, slope):
    listing = rank_bounds(count, slope)
    lot = jax.random.randint(jax.random.fold_in(key, 1), extent, 0, int(listing[count - 1]))
    standing = jnp.searchsorted(jnp.asarray(listing, jnp.int32), lot, side="right")
    return jax.random.permutation(jax.random.fold_in(key, 2), count)[standing].astype(jnp.int32)


def setup_inputs(seed: int = 0, part: int = 0) -> dict:
    key_list = jax.random.split(jax.random.key(seed), 12)
    part_splits = jax.random.split(jax.random.fold_in(key_list[11], part), 12)
    queries = draw_queries(jax.random.fold_in(jax.random.fold_in(key_list[11], part), 71), part)
    suffix_kv = draw_suffix_kv(jax.random.fold_in(jax.random.fold_in(key_list[11], part), 71), part)
    own_cache = draw_own_cache(jax.random.fold_in(jax.random.fold_in(key_list[11], part), 71), part)
    ctx_len = draw_ctx_len(jax.random.fold_in(jax.random.fold_in(key_list[11], part), 71), part)
    prefix_cache = draw_prefix_cache(jax.random.fold_in(jax.random.fold_in(key_list[11], part), 71), part)
    owners = draw_owners(jax.random.fold_in(jax.random.fold_in(key_list[11], part), 71), part)
    readers = plant(ranked(part_splits[6], (N_REPLICA,), NP, 2), jax.random.fold_in(part_splits[6], 3), 0, NP - 1).astype(jnp.int32)
    kv_pool = draw_kv_pool(jax.random.fold_in(jax.random.fold_in(key_list[11], part), 71), part)
    mig_target = draw_mig_target(jax.random.fold_in(jax.random.fold_in(key_list[11], part), 71), part)
    mig_block = jax.vmap(lambda own: jax.random.permutation(own, NB))(jax.random.split(part_splits[9], N_REPLICA)).reshape((N_REPLICA, NB)).astype(jnp.int32)
    mig_count = draw_mig_count(jax.random.fold_in(jax.random.fold_in(key_list[11], part), 71), part)
    return {"queries": queries, "suffix_kv": suffix_kv, "own_cache": own_cache, "ctx_len": ctx_len, "prefix_cache": prefix_cache, "owners": owners, "readers": readers, "kv_pool": kv_pool, "mig_target": mig_target, "mig_block": mig_block, "mig_count": mig_count}


def reference(queries, suffix_kv, own_cache, ctx_len, prefix_cache, owners, readers, kv_pool, mig_target, mig_block, mig_count):
    prefixes = prefix_cache.reshape(N_REPLICA, PL, 2 * HD)
    pools = kv_pool.reshape(N_REPLICA, NB, BLK, 2 * HD)
    owned = own_cache.reshape(N_REPLICA, CTX, 2 * HD)
    suffixes = suffix_kv.reshape(N_REPLICA, SUF, 2 * HD)
    query_sets = queries.reshape(N_REPLICA, SUF * HQ, HD)
    entries = jnp.arange(N_REPLICA, dtype=jnp.int32)
    source_ids = jnp.arange(N_REPLICA, dtype=jnp.int32)
    entry_live = entries[None, :] < mig_count[:, None]
    row_count = SUF * HQ
    positions = jnp.arange(row_count, dtype=jnp.int32) // HQ
    score_scale = HD ** -0.5

    def attend_replica(replica):
        prefix_rows = prefixes[owners[readers[replica]]]
        matching = (mig_target == replica) & entry_live
        entry_pos = jnp.sum(jnp.where(matching, entries[None, :], 0), axis=1).astype(jnp.int32)
        received = jnp.any(matching, axis=1)
        block_ids = jnp.take_along_axis(mig_block, entry_pos[:, None], axis=1)[:, 0]
        moved = pools[source_ids, block_ids].reshape(N_REPLICA * BLK, 2 * HD)
        moved_mask = jnp.repeat(received, BLK)
        own_rows = owned[replica]
        own_mask = jnp.arange(CTX, dtype=jnp.int32) < ctx_len[replica]
        suffix_rows = suffixes[replica]
        key_values = jnp.concatenate([prefix_rows, moved, own_rows, suffix_rows], axis=0)
        column_mask = jnp.concatenate([jnp.ones((PL,), bool), moved_mask, own_mask, jnp.ones((SUF,), bool)])
        causal = jnp.arange(SUF, dtype=jnp.int32)[None, :] <= positions[:, None]
        allowed = jnp.concatenate([jnp.ones((row_count, PL + N_REPLICA * BLK + CTX), bool), causal], axis=1)
        allowed = allowed & column_mask[None, :]
        scores = lax.dot_general(query_sets[replica], key_values[:, :HD], (((1,), (1,)), ((), ())), preferred_element_type=jnp.float32) * score_scale
        scores = jnp.where(allowed, scores, -jnp.inf)
        row_max = jnp.max(scores, axis=1, keepdims=True)
        exponent = jnp.exp(scores - row_max)
        denominator = jnp.sum(exponent, axis=1, keepdims=True)
        numerator = jnp.dot(exponent.astype(jnp.bfloat16), key_values[:, HD:], preferred_element_type=jnp.float32)
        return (numerator / denominator).astype(jnp.bfloat16).reshape(SUF, HQ * HD)

    attended = lax.map(attend_replica, jnp.arange(N_REPLICA, dtype=jnp.int32))
    return attended.reshape(N_REPLICA * SUF, HQ * HD)
```

```python
import functools
import math

import jax
import jax.numpy as jnp
from jax import lax
from jax.experimental import pallas as pl
from jax.experimental.pallas import tpu as pltpu
from jax.sharding import PartitionSpec as P

DEAD = 64.0
LIMIT = 32.0
MESH = pl.DeviceIdType.MESH


def attention_kernel(
    cfg,
    meta_ref,
    q_ref,
    suffix_ref,
    own_ref,
    prefix_ref,
    out_blocks,
    o_ref,
    gathered,
    first_recv,
    later_recv,
    arrived,
    m_ref,
    l_ref,
    acc_ref,
    rs_send,
    rs_recv,
    ag_send,
    ag_recv,
    st_send,
    st_recv,
    mv_send,
    mv_recv,
    local_sem,
    ready,
):
    replicas, prefixes, heads, hd = cfg
    steps = replicas.bit_length() - 1
    prefix_len = prefix_ref.shape[0]
    parts = 2
    part_rows = prefix_len // parts
    piece = part_rows // replicas
    dynamic = prefixes - 1
    orders = [list(range(steps)), list(range(steps))]
    if steps > 2:
        orders[1][1], orders[1][2] = orders[1][2], orders[1][1]
    me = lax.axis_index("replica")
    coef = hd ** (-0.5) * math.log2(math.e)

    def bit_of(device, b):
        return lax.rem(device // (1 << b), 2)

    def partner(b):
        return me + (1 - 2 * bit_of(me, b)) * (1 << b)

    def range_low(device, part, level):
        low = part * part_rows
        for t in range(level):
            low = low + bit_of(device, orders[part][t]) * (part_rows >> (t + 1))
        return low

    def rows_at(low, count):
        return pl.ds(pl.multiple_of(low, piece), count)

    barrier = pltpu.get_barrier_semaphore()

    def greet(i, c):
        pl.semaphore_signal(
            barrier, inc=1, device_id={"replica": lax.rem(me + i, replicas)}, device_id_type=MESH
        )
        return c

    lax.fori_loop(1, replicas, greet, 0)
    pl.semaphore_wait(barrier, replicas - 1)

    def rs_copy(t, part):
        b = orders[part][t]
        rows = part_rows >> (t + 1)
        low = range_low(me, part, t) + (1 - bit_of(me, b)) * rows
        if t == 0:
            src = prefix_ref.at[rows_at(low, rows), :]
            dst = first_recv.at[part]
        else:
            src = gathered.at[pl.ds(0, dynamic), rows_at(low, rows), :]
            dst = later_recv.at[part, :, pl.ds((part_rows >> 1) - 2 * rows, rows), :]
        return pltpu.make_async_remote_copy(
            src_ref=src,
            dst_ref=dst,
            send_sem=rs_send.at[t, part],
            recv_sem=rs_recv.at[t, part],
            device_id={"replica": partner(b)},
            device_id_type=MESH,
        )

    def rs_take(t, part):
        b = orders[part][t]
        rows = part_rows >> (t + 1)
        low = range_low(me, part, t) + bit_of(me, b) * rows
        for d in range(dynamic):
            other = bit_of(meta_ref[d], b) != bit_of(me, b)
            if t == 0:
                mine = prefix_ref[rows_at(low, rows), :]
                theirs = first_recv[part]
            else:
                mine = gathered[d, rows_at(low, rows), :]
                theirs = later_recv[part, d, pl.ds((part_rows >> 1) - 2 * rows, rows), :]
            gathered[d, rows_at(low, rows), :] = jnp.where(other, theirs, mine)

    def ag_copy(t, part):
        b = orders[part][t]
        rows = part_rows >> (t + 1)
        view = gathered.at[:, rows_at(range_low(me, part, t + 1), rows), :]
        return pltpu.make_async_remote_copy(
            src_ref=view,
            dst_ref=view,
            send_sem=ag_send.at[t, part],
            recv_sem=ag_recv.at[t, part],
            device_id={"replica": partner(b)},
            device_id_type=MESH,
        )

    def ag_start(t, part):
        if t > 0:
            pl.semaphore_wait(ready.at[t, part], 1)
        ag_copy(t, part).start()

    def scatter_copy(target, part):
        low = range_low(target, part, steps)
        return pltpu.make_async_remote_copy(
            src_ref=prefix_ref.at[rows_at(low, piece), :],
            dst_ref=gathered.at[prefixes - 1, rows_at(low, piece), :],
            send_sem=st_send.at[target, part],
            recv_sem=st_recv.at[part],
            device_id={"replica": target},
            device_id_type=MESH,
        )

    def move_copy(k):
        odd = lax.rem(k, 2)
        offset = odd * ((k + 1) // 2) + (1 - odd) * (replicas - k // 2)
        target = lax.rem(me + offset, replicas)
        return pltpu.make_async_remote_copy(
            src_ref=out_blocks.at[target],
            dst_ref=arrived.at[k],
            send_sem=mv_send.at[k],
            recv_sem=mv_recv.at[k],
            device_id={"replica": target},
            device_id_type=MESH,
        )

    for part in range(parts):
        rs_copy(0, part).start()

    @pl.when(me == replicas - 1)
    def _():
        def send(target, c):
            for part in range(parts):
                scatter_copy(target, part).start()
            return c

        lax.fori_loop(0, replicas - 1, send, 0)
        for part in range(parts):
            low = range_low(me, part, steps)
            gathered[prefixes - 1, rows_at(low, piece), :] = prefix_ref[rows_at(low, piece), :]

    def send_block(k, c):
        move_copy(k).start()
        return c

    lax.fori_loop(1, replicas, send_block, 0)
    local = pltpu.make_async_copy(out_blocks.at[me], arrived.at[0], local_sem)
    local.start()

    m_ref[...] = jnp.full_like(m_ref, -jnp.inf)
    l_ref[...] = jnp.zeros_like(l_ref)
    acc_ref[...] = jnp.zeros_like(acc_ref)

    def attend(load, mask_of=None):
        key_value = load()
        count = key_value.shape[0]
        mask = None if mask_of is None else mask_of()

        def one_head(h, c):
            q = q_ref[:, pl.ds(pl.multiple_of(h * hd, hd), hd)]
            scores = lax.dot_general(
                q, key_value[:, :hd], (((1,), (1,)), ((), ())), preferred_element_type=jnp.float32
            )
            if mask is not None:
                scores = jnp.where(mask, scores, -jnp.inf)
            before = m_ref[h]
            new_max = jnp.maximum(before, jnp.max(scores, axis=1, keepdims=True))
            shrink = jnp.exp2((before - new_max) * coef)
            total = l_ref[h] * shrink
            top = new_max * coef
            weights = []
            for g in range(count // hd):
                w = jnp.exp2(scores[:, g * hd : (g + 1) * hd] * coef - top)
                total = total + w
                weights.append(w.astype(jnp.bfloat16))
            l_ref[h] = total
            m_ref[h] = new_max
            acc_ref[h] = acc_ref[h] * shrink + jnp.dot(
                jnp.concatenate(weights, axis=1),
                key_value[:, hd:],
                preferred_element_type=jnp.float32,
            )
            return c

        lax.fori_loop(0, heads, one_head, 0, unroll=2)

    def attend_suffix():
        n = suffix_ref.shape[0]
        causal = lambda: (
            lax.broadcasted_iota(jnp.int32, (n, n), 1) <= lax.broadcasted_iota(jnp.int32, (n, n), 0)
        )
        attend(lambda: suffix_ref[...], causal)

    def attend_own():
        n = own_ref.shape[0]
        attend(
            lambda: own_ref[...],
            lambda: lax.broadcasted_iota(jnp.int32, (1, n), 1) < meta_ref[dynamic],
        )

    block = arrived.shape[1]
    chunk = 8

    def attend_moved(first):
        for k in range(first, first + chunk):
            if k == 0:
                local.wait()
            else:
                move_copy(k).wait_recv()
        attend(
            lambda: arrived[pl.ds(first, chunk)].reshape(chunk * block, 2 * hd),
            lambda: jnp.concatenate(
                [
                    jnp.concatenate(
                        [arrived[k, 0:16, 0:hd].astype(jnp.float32)[0:1]] * (block // hd), axis=1
                    )
                    for k in range(first, first + chunk)
                ],
                axis=1,
            )
            < LIMIT,
        )

    slot = meta_ref[dynamic + 1]

    def attend_prefix(low, rows):
        def load():
            key_value = gathered[0, rows_at(low, rows), :]
            for p in range(1, prefixes):
                key_value = jnp.where(slot == p, gathered[p, rows_at(low, rows), :], key_value)
            return key_value

        attend(load)

    for t in range(steps):
        if t == 0:
            attend_suffix()
        if t == 1:
            attend_own()
        for part in range(parts):
            rs_copy(t, part).wait()
            if t > 0:
                pl.semaphore_signal(
                    ready.at[t, part],
                    inc=1,
                    device_id={"replica": partner(orders[part][t])},
                    device_id_type=MESH,
                )
            rs_take(t, part)
            if t + 1 < steps:
                rs_copy(t + 1, part).start()

    @pl.when(me != replicas - 1)
    def _():
        for part in range(parts):
            scatter_copy(me, part).wait_recv()

    moved_groups = list(range(0, replicas, chunk))
    for part in range(parts):
        ag_start(steps - 1, part)
    for t in range(steps - 1, 0, -1):
        if t < 3 and len(moved_groups) > 2:
            attend_moved(moved_groups.pop(0))
        for part in range(parts):
            ag_copy(t, part).wait()
            ag_start(t - 1, part)
    for part in range(parts):
        attend_prefix(range_low(me, part, 1), part_rows // 2)
    while len(moved_groups) > 1:
        attend_moved(moved_groups.pop(0))
    for part in range(parts):
        ag_copy(0, part).wait()
        other = part * part_rows + (1 - bit_of(me, orders[part][0])) * (part_rows // 2)
        attend_prefix(other, part_rows // 2)
    while moved_groups:
        attend_moved(moved_groups.pop(0))

    for h in range(heads):
        denominator = jnp.sum(l_ref[h], axis=1, keepdims=True)
        o_ref[:, h * hd : (h + 1) * hd] = (acc_ref[h] / denominator).astype(o_ref.dtype)

    def sent(k, c):
        move_copy(k).wait_send()
        return c

    lax.fori_loop(1, replicas, sent, 0)

    @pl.when(me == replicas - 1)
    def _():
        def done(target, c):
            for part in range(parts):
                scatter_copy(target, part).wait_send()
            return c

        lax.fori_loop(0, replicas - 1, done, 0)


def on_device(
    queries,
    suffix_kv,
    own_cache,
    ctx_len,
    prefix_cache,
    owners,
    readers,
    kv_pool,
    mig_target,
    mig_block,
    mig_count,
):
    replicas = lax.axis_size("replica")
    me = lax.axis_index("replica")
    hd = suffix_kv.shape[1] // 2
    heads = queries.shape[1] // hd
    tokens = queries.shape[0]
    prefixes = owners.shape[0]
    targets = mig_target[0]
    block_ids = mig_block[0]
    entry_live = jnp.arange(targets.shape[0], dtype=jnp.int32) < mig_count[0]
    matching = (targets[None, :] == jnp.arange(replicas, dtype=jnp.int32)[:, None]) & entry_live[
        None, :
    ]
    slot_ids = jnp.sum(jnp.where(matching, block_ids[None, :], 0), axis=1)
    live = jnp.any(matching, axis=1)
    outgoing = jnp.where(live[:, None, None], kv_pool[slot_ids], jnp.bfloat16(DEAD))

    is_last = owners == replicas - 1
    last_at = jnp.sum(jnp.where(is_last, jnp.arange(prefixes, dtype=jnp.int32), 0))
    index = jnp.arange(prefixes - 1, dtype=jnp.int32)
    source = index + (index >= last_at)
    dynamic_owners = jnp.sum(
        jnp.where(
            source[:, None] == jnp.arange(prefixes, dtype=jnp.int32)[None, :], owners[None, :], 0
        ),
        axis=1,
    )
    mine = jnp.sum(jnp.where(jnp.arange(replicas, dtype=jnp.int32) == me, readers, 0))
    slot = jnp.where(mine == last_at, prefixes - 1, mine - (mine > last_at))
    meta = jnp.concatenate([dynamic_owners, ctx_len, slot[None]]).astype(jnp.int32)

    steps = replicas.bit_length() - 1
    prefix_len, width = prefix_cache.shape
    part_rows = prefix_len // 2
    vmem = pl.BlockSpec(memory_space=pltpu.VMEM)
    dma = pltpu.SemaphoreType.DMA
    return pl.pallas_call(
        functools.partial(attention_kernel, (replicas, prefixes, heads, hd)),
        out_shape=jax.ShapeDtypeStruct(queries.shape, jnp.bfloat16),
        in_specs=[
            pl.BlockSpec(memory_space=pltpu.SMEM),
            vmem,
            vmem,
            vmem,
            vmem,
            pl.BlockSpec(memory_space=pl.ANY),
        ],
        out_specs=vmem,
        scratch_shapes=[
            pltpu.VMEM((prefixes, prefix_len, width), jnp.bfloat16),
            pltpu.VMEM((2, part_rows // 2, width), jnp.bfloat16),
            pltpu.VMEM((2, prefixes - 1, part_rows // 2, width), jnp.bfloat16),
            pltpu.VMEM((replicas,) + kv_pool.shape[1:], jnp.bfloat16),
            pltpu.VMEM((heads, tokens, hd), jnp.float32),
            pltpu.VMEM((heads, tokens, hd), jnp.float32),
            pltpu.VMEM((heads, tokens, hd), jnp.float32),
            dma((steps, 2)),
            dma((steps, 2)),
            dma((steps, 2)),
            dma((steps, 2)),
            dma((replicas, 2)),
            dma((2,)),
            dma((replicas,)),
            dma((replicas,)),
            dma,
            pltpu.SemaphoreType.REGULAR((steps, 2)),
        ],
        compiler_params=pltpu.CompilerParams(
            collective_id=0, has_side_effects=True, vmem_limit_bytes=56 * 1024 * 1024
        ),
    )(meta, queries, suffix_kv, own_cache, prefix_cache, outgoing)


def solution(mesh):
    in_specs = (
        P(("groups", "replica"), None),
        P(("groups", "replica"), None),
        P(("groups", "replica"), None),
        P(("groups", "replica")),
        P(("groups", "replica"), None),
        P("groups"),
        P("groups"),
        P(("groups", "replica"), None, None),
        P(("groups", "replica"), None),
        P(("groups", "replica"), None),
        P(("groups", "replica")),
    )
    out_specs = P(("groups", "replica"), None)
    return jax.shard_map(
        on_device, mesh=mesh, in_specs=in_specs, out_specs=out_specs, check_vma=False
    )
```

```python
import functools
import math

import jax
import jax.numpy as jnp
from jax import lax
from jax.experimental import pallas as pl
from jax.experimental.pallas import tpu as pltpu
from jax.sharding import PartitionSpec as P

DEAD = 64.0
LIMIT = 32.0
MESH = pl.DeviceIdType.MESH


def attention_kernel(
    cfg,
    meta_ref,
    q_ref,
    suffix_ref,
    own_ref,
    prefix_ref,
    pool_ref,
    o_ref,
    gathered,
    first_recv,
    later_recv,
    arrived,
    out_blocks,
    m_ref,
    l_ref,
    acc_ref,
    rs_send,
    rs_recv,
    ag_send,
    ag_recv,
    st_send,
    st_recv,
    mv_send,
    mv_recv,
    core_send,
    core_recv,
    ready,
):
    replicas, prefixes, heads, hd = cfg
    steps = replicas.bit_length() - 1
    prefix_len = prefix_ref.shape[0]
    parts = 2
    part_rows = prefix_len // parts
    piece = part_rows // replicas
    dynamic = prefixes - 1
    orders = [list(range(steps)), list(range(steps))]
    if steps > 2:
        orders[1][1], orders[1][2] = orders[1][2], orders[1][1]
    me = lax.axis_index("replica")
    coef = hd ** (-0.5) * math.log2(math.e)

    def bit_of(device, b):
        return lax.rem(device // (1 << b), 2)

    def partner(b):
        return me + (1 - 2 * bit_of(me, b)) * (1 << b)

    def range_low(device, part, level):
        low = part * part_rows
        for t in range(level):
            low = low + bit_of(device, orders[part][t]) * (part_rows >> (t + 1))
        return low

    def rows_at(low, count):
        return pl.ds(pl.multiple_of(low, piece), count)

    barrier = pltpu.get_barrier_semaphore()

    def greet(i, c):
        pl.semaphore_signal(
            barrier, inc=1, device_id={"replica": lax.rem(me + i, replicas)}, device_id_type=MESH
        )
        return c

    lax.fori_loop(1, replicas, greet, 0)
    pl.semaphore_wait(barrier, replicas - 1)

    def rs_copy(t, part):
        b = orders[part][t]
        rows = part_rows >> (t + 1)
        low = range_low(me, part, t) + (1 - bit_of(me, b)) * rows
        if t == 0:
            src = prefix_ref.at[rows_at(low, rows), :]
            dst = first_recv.at[part]
        else:
            src = gathered.at[pl.ds(0, dynamic), rows_at(low, rows), :]
            dst = later_recv.at[part, :, pl.ds((part_rows >> 1) - 2 * rows, rows), :]
        return pltpu.make_async_remote_copy(
            src_ref=src,
            dst_ref=dst,
            send_sem=rs_send.at[t, part],
            recv_sem=rs_recv.at[t, part],
            device_id={"replica": partner(b)},
            device_id_type=MESH,
        )

    def rs_take(t, part):
        b = orders[part][t]
        rows = part_rows >> (t + 1)
        low = range_low(me, part, t) + bit_of(me, b) * rows
        for d in range(dynamic):
            other = bit_of(meta_ref[d], b) != bit_of(me, b)
            if t == 0:
                mine = prefix_ref[rows_at(low, rows), :]
                theirs = first_recv[part]
            else:
                mine = gathered[d, rows_at(low, rows), :]
                theirs = later_recv[part, d, pl.ds((part_rows >> 1) - 2 * rows, rows), :]
            gathered[d, rows_at(low, rows), :] = jnp.where(other, theirs, mine)

    def ag_copy(t, part):
        b = orders[part][t]
        rows = part_rows >> (t + 1)
        view = gathered.at[:, rows_at(range_low(me, part, t + 1), rows), :]
        return pltpu.make_async_remote_copy(
            src_ref=view,
            dst_ref=view,
            send_sem=ag_send.at[t, part],
            recv_sem=ag_recv.at[t, part],
            device_id={"replica": partner(b)},
            device_id_type=MESH,
        )

    def quarter(device, part, taken):
        b = orders[part][1]
        side = bit_of(device, b) if taken == 0 else 1 - bit_of(device, b)
        return range_low(device, part, 1) + side * (part_rows >> 2)

    def core_copy(taken, part):
        view = gathered.at[:, rows_at(quarter(me, part, taken), part_rows >> 2), :]
        return pltpu.make_async_remote_copy(
            src_ref=view,
            dst_ref=view,
            send_sem=core_send.at[taken, part],
            recv_sem=core_recv.at[taken, part],
            device_id={"replica": partner(orders[part][0])},
            device_id_type=MESH,
        )

    def ag_start(t, part):
        if t > 0:
            pl.semaphore_wait(ready.at[t, part], 1)
        ag_copy(t, part).start()

    def scatter_copy(target, part):
        low = range_low(target, part, steps)
        return pltpu.make_async_remote_copy(
            src_ref=prefix_ref.at[rows_at(low, piece), :],
            dst_ref=gathered.at[prefixes - 1, rows_at(low, piece), :],
            send_sem=st_send.at[target, part],
            recv_sem=st_recv.at[part],
            device_id={"replica": target},
            device_id_type=MESH,
        )

    def move_copy(k):
        odd = lax.rem(k, 2)
        offset = odd * ((k + 1) // 2) + (1 - odd) * (replicas - k // 2)
        target = lax.rem(me + offset, replicas)
        return pltpu.make_async_remote_copy(
            src_ref=out_blocks.at[target],
            dst_ref=arrived.at[k],
            send_sem=mv_send.at[k],
            recv_sem=mv_recv.at[k],
            device_id={"replica": target},
            device_id_type=MESH,
        )

    for part in range(parts):
        rs_copy(0, part).start()

    @pl.when(me == replicas - 1)
    def _():
        def send(target, c):
            for part in range(parts):
                scatter_copy(target, part).start()
            return c

        lax.fori_loop(0, replicas - 1, send, 0)
        for part in range(parts):
            low = range_low(me, part, steps)
            gathered[prefixes - 1, rows_at(low, piece), :] = prefix_ref[rows_at(low, piece), :]

    def picked(target):
        code = meta_ref[dynamic + 2 + target]
        block = pool_ref[jnp.maximum(code, 0)]
        return jnp.where(code >= 0, block, jnp.full_like(block, DEAD))

    def send_block(k, c):
        odd = lax.rem(k, 2)
        offset = odd * ((k + 1) // 2) + (1 - odd) * (replicas - k // 2)
        target = lax.rem(me + offset, replicas)
        out_blocks[target] = picked(target)
        move_copy(k).start()
        return c

    lax.fori_loop(1, replicas, send_block, 0)
    arrived[0] = picked(me)

    m_ref[...] = jnp.full_like(m_ref, -jnp.inf)
    l_ref[...] = jnp.zeros_like(l_ref)
    acc_ref[...] = jnp.zeros_like(acc_ref)

    def attend(load, mask_of=None):
        key_value = load()
        count = key_value.shape[0]
        mask = None if mask_of is None else mask_of()

        def one_head(h, c):
            q = q_ref[:, pl.ds(pl.multiple_of(h * hd, hd), hd)]
            scores = lax.dot_general(
                q, key_value[:, :hd], (((1,), (1,)), ((), ())), preferred_element_type=jnp.float32
            )
            if mask is not None:
                scores = jnp.where(mask, scores, -jnp.inf)
            before = m_ref[h]
            new_max = jnp.maximum(before, jnp.max(scores, axis=1, keepdims=True))
            shrink = jnp.exp2((before - new_max) * coef)
            total = l_ref[h] * shrink
            top = new_max * coef
            weights = []
            for g in range(count // hd):
                w = jnp.exp2(scores[:, g * hd : (g + 1) * hd] * coef - top)
                total = total + w
                weights.append(w.astype(jnp.bfloat16))
            l_ref[h] = total
            m_ref[h] = new_max
            acc_ref[h] = acc_ref[h] * shrink + jnp.dot(
                jnp.concatenate(weights, axis=1),
                key_value[:, hd:],
                preferred_element_type=jnp.float32,
            )
            return c

        lax.fori_loop(0, heads, one_head, 0, unroll=2)

    def attend_suffix():
        n = suffix_ref.shape[0]
        causal = lambda: (
            lax.broadcasted_iota(jnp.int32, (n, n), 1) <= lax.broadcasted_iota(jnp.int32, (n, n), 0)
        )
        attend(lambda: suffix_ref[...], causal)

    def attend_own():
        n = own_ref.shape[0]
        attend(
            lambda: own_ref[...],
            lambda: lax.broadcasted_iota(jnp.int32, (1, n), 1) < meta_ref[dynamic],
        )

    block = arrived.shape[1]
    chunk = 8

    def attend_moved(first):
        for k in range(first, first + chunk):
            if k > 0:
                move_copy(k).wait_recv()
        attend(
            lambda: arrived[pl.ds(first, chunk)].reshape(chunk * block, 2 * hd),
            lambda: jnp.concatenate(
                [
                    jnp.concatenate(
                        [arrived[k, 0:16, 0:hd].astype(jnp.float32)[0:1]] * (block // hd), axis=1
                    )
                    for k in range(first, first + chunk)
                ],
                axis=1,
            )
            < LIMIT,
        )

    slot = meta_ref[dynamic + 1]

    def attend_prefix(low, rows):
        def load():
            key_value = gathered[0, rows_at(low, rows), :]
            for p in range(1, prefixes):
                key_value = jnp.where(slot == p, gathered[p, rows_at(low, rows), :], key_value)
            return key_value

        attend(load)

    for t in range(steps):
        if t == 0:
            attend_suffix()
        if t == 1:
            attend_own()
        for part in range(parts):
            rs_copy(t, part).wait()
            if t > 0:
                pl.semaphore_signal(
                    ready.at[t, part],
                    inc=1,
                    device_id={"replica": partner(orders[part][t])},
                    device_id_type=MESH,
                )
            rs_take(t, part)
            if t + 1 < steps:
                rs_copy(t + 1, part).start()

    @pl.when(me != replicas - 1)
    def _():
        for part in range(parts):
            scatter_copy(me, part).wait_recv()

    moved_groups = list(range(0, replicas, chunk))
    quarter_rows = part_rows >> 2
    beside = partner(orders[0][0])
    for part in range(parts):
        ag_start(steps - 1, part)
    for t in range(steps - 1, 1, -1):
        if t == 2:
            attend_moved(moved_groups.pop(0))
        for part in range(parts):
            ag_copy(t, part).wait()
            ag_start(t - 1, part)
            if t == 2:
                core_copy(0, part).start()
    for part in range(parts):
        attend_prefix(quarter(me, part, 0), quarter_rows)
    for part in range(parts):
        core_copy(0, part).wait()
        attend_prefix(quarter(beside, part, 0), quarter_rows)
    for part in range(parts):
        ag_copy(1, part).wait()
        core_copy(1, part).start()
    for part in range(parts):
        attend_prefix(quarter(me, part, 1), quarter_rows)
    for part in range(parts):
        core_copy(1, part).wait()
        attend_prefix(quarter(beside, part, 1), quarter_rows)
    while moved_groups:
        attend_moved(moved_groups.pop(0))

    for h in range(heads):
        denominator = jnp.sum(l_ref[h], axis=1, keepdims=True)
        o_ref[:, h * hd : (h + 1) * hd] = (acc_ref[h] / denominator).astype(o_ref.dtype)

    def sent(k, c):
        move_copy(k).wait_send()
        return c

    lax.fori_loop(1, replicas, sent, 0)

    @pl.when(me == replicas - 1)
    def _():
        def done(target, c):
            for part in range(parts):
                scatter_copy(target, part).wait_send()
            return c

        lax.fori_loop(0, replicas - 1, done, 0)


def on_device(
    queries,
    suffix_kv,
    own_cache,
    ctx_len,
    prefix_cache,
    owners,
    readers,
    kv_pool,
    mig_target,
    mig_block,
    mig_count,
):
    replicas = lax.axis_size("replica")
    me = lax.axis_index("replica")
    hd = suffix_kv.shape[1] // 2
    heads = queries.shape[1] // hd
    tokens = queries.shape[0]
    prefixes = owners.shape[0]
    targets = mig_target[0]
    block_ids = mig_block[0]
    entry_live = jnp.arange(targets.shape[0], dtype=jnp.int32) < mig_count[0]
    matching = (targets[None, :] == jnp.arange(replicas, dtype=jnp.int32)[:, None]) & entry_live[
        None, :
    ]
    codes = jnp.sum(jnp.where(matching, block_ids[None, :] + 1, 0), axis=1) - 1

    is_last = owners == replicas - 1
    last_at = jnp.sum(jnp.where(is_last, jnp.arange(prefixes, dtype=jnp.int32), 0))
    index = jnp.arange(prefixes - 1, dtype=jnp.int32)
    source = index + (index >= last_at)
    dynamic_owners = jnp.sum(
        jnp.where(
            source[:, None] == jnp.arange(prefixes, dtype=jnp.int32)[None, :], owners[None, :], 0
        ),
        axis=1,
    )
    mine = jnp.sum(jnp.where(jnp.arange(replicas, dtype=jnp.int32) == me, readers, 0))
    slot = jnp.where(mine == last_at, prefixes - 1, mine - (mine > last_at))
    meta = jnp.concatenate([dynamic_owners, ctx_len, slot[None], codes]).astype(jnp.int32)

    steps = replicas.bit_length() - 1
    prefix_len, width = prefix_cache.shape
    part_rows = prefix_len // 2
    vmem = pl.BlockSpec(memory_space=pltpu.VMEM)
    dma = pltpu.SemaphoreType.DMA
    return pl.pallas_call(
        functools.partial(attention_kernel, (replicas, prefixes, heads, hd)),
        out_shape=jax.ShapeDtypeStruct(queries.shape, jnp.bfloat16),
        in_specs=[
            pl.BlockSpec(memory_space=pltpu.SMEM),
            vmem,
            vmem,
            vmem,
            vmem,
            vmem,
        ],
        out_specs=vmem,
        scratch_shapes=[
            pltpu.VMEM((prefixes, prefix_len, width), jnp.bfloat16),
            pltpu.VMEM((2, part_rows // 2, width), jnp.bfloat16),
            pltpu.VMEM((2, prefixes - 1, part_rows // 2, width), jnp.bfloat16),
            pltpu.VMEM((replicas,) + kv_pool.shape[1:], jnp.bfloat16),
            pltpu.VMEM((replicas,) + kv_pool.shape[1:], jnp.bfloat16),
            pltpu.VMEM((heads, tokens, hd), jnp.float32),
            pltpu.VMEM((heads, tokens, hd), jnp.float32),
            pltpu.VMEM((heads, tokens, hd), jnp.float32),
            dma((steps, 2)),
            dma((steps, 2)),
            dma((steps, 2)),
            dma((steps, 2)),
            dma((replicas, 2)),
            dma((2,)),
            dma((replicas,)),
            dma((replicas,)),
            dma((2, 2)),
            dma((2, 2)),
            pltpu.SemaphoreType.REGULAR((steps, 2)),
        ],
        compiler_params=pltpu.CompilerParams(
            collective_id=0, has_side_effects=True, vmem_limit_bytes=56 * 1024 * 1024
        ),
    )(meta, queries, suffix_kv, own_cache, prefix_cache, kv_pool)


def solution(mesh):
    in_specs = (
        P(("groups", "replica"), None),
        P(("groups", "replica"), None),
        P(("groups", "replica"), None),
        P(("groups", "replica")),
        P(("groups", "replica"), None),
        P("groups"),
        P("groups"),
        P(("groups", "replica"), None, None),
        P(("groups", "replica"), None),
        P(("groups", "replica"), None),
        P(("groups", "replica")),
    )
    out_specs = P(("groups", "replica"), None)
    return jax.shard_map(
        on_device, mesh=mesh, in_specs=in_specs, out_specs=out_specs, check_vma=False
    )
```
